128 devices in a mesh: grp: 4 (over y), row: 32 (over z, x, core).
Axes of the slice: x: 4, y: 4, z: 4, core: 2. Of those that a mesh axis runs over, the one named last changes fastest.
Arguments:
- feats: bfloat16 [65536, 512], P(('grp', 'row')), may hold values from -6 to 6
- tile_vals: bfloat16 [12288, 128, 128], P(('grp', 'row')), may hold values from -0.1875 to 0.1875
- tile_rows: int32 [12288], P(('grp', 'row')), may hold values from 0 to 15, as said below
- tile_slots: int32 [12288], P(('grp', 'row')), may hold values from 0 to 31, as said below
- tile_count: int32 [128], P(('grp', 'row')), may hold values from 32 to 96, as said below
- send_list: int32 [128, 32, 1], P(('grp', 'row')), may hold values from 0 to 3
- w_in: bfloat16 [2, 512, 1024], replicated, may hold values from -0.25 to 0.25
- w_out: bfloat16 [2, 1024, 512], replicated, may hold values from -0.1875 to 0.1875
- cotangent: bfloat16 [65536, 512], P(('grp', 'row')), may hold values from -6 to 6
Outputs:
- feat_grad: bfloat16 [65536, 512], P(('grp', 'row'))
- w_in_grad: float32 [2, 512, 1024], P(None, ('grp', 'row'))
- w_out_grad: float32 [2, 1024, 512], P(None, ('grp', 'row'))
The draws below stay inside these ranges and needn't reach their ends.
Inputs may be any that keep to these rules, and one draw needn't show every extreme that they name: send_list[d, r, c] is the own block (0 to 3) that device d sends as its c-th to the device at row index r of its grp. p = tile_rows[d * 96 + t] names block p % 4 of the device at grp index p // 4 and d's row index; each of the 16 values stands among the first 16 tiles of every device. `tile_slots`: slot s is the block that the device at row index s of the same grp sends to this device; each of the 32 slots stands among the first 32 tiles of every device. Only the first tile_count[d] tiles of device d are used; at least one device uses all 96.
All inputs are finite; a program needn't handle non-finite values.
Results may differ from the reference program's by a relative error of at most 0.017.
Values may be sent and summed in bfloat16 or wider, within the bound.
No kernel may reach another device: no remote copies, remote signals or barrier semaphores. Data moves between devices by JAX's collectives and lax.ppermute only.
A program may use at most 128 MiB of HBM per device.

```python
import jax
import jax.numpy as jnp
from jax import lax

D = 512
FF = 1024
BLK = 128
TPR = 8
CAP = 1
LAYERS = 2
BPD = 4
SLOTS = 32
PANEL = 16
TMAX = 96
NODES = 65536
N_ROW = 32
DEVICES = 128


def covering_list(key, span):
    keys = jax.random.split(key, DEVICES)

    def per_device(device_key):
        first_key, other_key = jax.random.split(device_key)
        first_part = jax.random.permutation(first_key, span).astype(jnp.int32)
        first_part = jnp.pad(first_part, (0, TMAX - span))
        remaining = jax.random.randint(other_key, (TMAX,), 0, span, dtype=jnp.int32)
        return jnp.where(jnp.arange(TMAX, dtype=jnp.int32) < span, first_part, remaining)
    return jax.vmap(per_device)(keys).reshape(DEVICES * TMAX)


def draw_tile_rows(key, part):
    return covering_list(jax.random.fold_in(key, 11), PANEL)


def draw_tile_slots(key, part):
    return covering_list(jax.random.fold_in(key, 23), SLOTS)


def draw_tile_count(key, part):
    count_key, busy_key = jax.random.split(jax.random.fold_in(key, 37))
    base_count = jax.random.randint(count_key, (DEVICES,), TPR * BPD, TPR * BPD * 3 // 2 + 1, dtype=jnp.int32)
    busy_mask = jax.random.permutation(busy_key, DEVICES) < max(1, DEVICES // 16)
    return jnp.where(busy_mask, TMAX, base_count).astype(jnp.int32)


def touch_ends(result, key, smallest, high):
    spot = [jax.random.randint(jax.random.fold_in(key, axis), (), 0, length) for axis, length in enumerate(result.shape)]
    main_axis = result.shape.index(max(result.shape))
    neighbour = spot[:main_axis] + [(spot[main_axis] + 1) % result.shape[main_axis]] + spot[main_axis + 1:]
    return result.at[tuple(spot)].set(smallest).at[tuple(neighbour)].set(high)


def level_of(rng, dims, cuts, least, largest):
    def one(position, shards_of):
        heights = jax.random.uniform(jax.random.fold_in(jax.random.fold_in(rng, 6), position), (shards_of,), jnp.float32, least / len(cuts), largest / len(cuts))
        return jnp.repeat(jnp.exp(heights), dims[position] // shards_of).reshape((-1,) + (1,) * (len(dims) - position - 1))

    level = one(*cuts[0])
    for cut in cuts[1:]:
        level = level * one(*cut)
    return level


def centred(stream_key, dims, deviation, bound, cuts=(), held_as=jnp.bfloat16):
    factor_of = level_of(stream_key, dims, cuts, -0.22, 0.18) if cuts else 1.0
    result = jax.random.normal(stream_key, dims, jnp.float32) * deviation * factor_of
    return jnp.minimum(jnp.maximum(result, -bound), bound).astype(held_as)


def setup_inputs(seed: int = 0) -> dict:
    seeds = jax.random.split(jax.random.key(seed), 10)
    feats = centred(seeds[0], (NODES, D), 1.0, 6.0, ((0, 128),))
    tile_vals = centred(seeds[1], (DEVICES * TMAX, BLK, BLK), (TPR * BLK) ** -0.5, 0.1875, ((0, 128),))
    tile_rows = draw_tile_rows(jax.random.fold_in(seeds[9], 71), 0)
    tile_slots = draw_tile_slots(jax.random.fold_in(seeds[9], 71), 0)
    tile_count = draw_tile_count(jax.random.fold_in(seeds[9], 71), 0)
    send_list = touch_ends(jax.random.randint(seeds[5], (DEVICES, N_ROW, CAP), 0, BPD), jax.random.fold_in(seeds[5], 1), 0, BPD - 1).astype(jnp.int32)
    w_in = centred(seeds[6], (LAYERS, D, FF), D ** -0.5, 0.25)
    w_out = centred(seeds[7], (LAYERS, FF, D), FF ** -0.5, 0.1875)
    cotangent = centred(seeds[8], (NODES, D), 1.0, 6.0, ((0, 128),))
    return {"feats": feats, "tile_vals": tile_vals, "tile_rows": tile_rows, "tile_slots": tile_slots, "tile_count": tile_count, "send_list": send_list, "w_in": w_in, "w_out": w_out, "cotangent": cotangent}


eps = 1e-06

def tile_maps(tile_rows, tile_slots, tile_count, send_list):
    device_ids = jnp.arange(DEVICES, dtype=jnp.int32)
    grp_index = device_ids // N_ROW
    row_index = device_ids % N_ROW
    row_ids = tile_rows.reshape(DEVICES, TMAX)
    slot_ids = tile_slots.reshape(DEVICES, TMAX)
    owner = row_ids // BPD * N_ROW + row_index[:, None]
    row_block = (owner * BPD + row_ids % BPD).astype(jnp.int32)
    slot_range = jnp.arange(SLOTS, dtype=jnp.int32)
    sender = grp_index[:, None] * N_ROW + slot_range[None, :] // CAP
    picked = send_list[sender, row_index[:, None], slot_range[None, :] % CAP]
    slot_block = (sender * BPD + picked).astype(jnp.int32)
    col_block = jnp.take_along_axis(slot_block, slot_ids, axis=1).astype(jnp.int32)
    live_mask = (jnp.arange(TMAX, dtype=jnp.int32)[None, :] < tile_count[:, None]).astype(jnp.float32)
    return (row_block, col_block, slot_ids, slot_block, live_mask)

def aggregate(blocks, tiles, row_block, col_block, live_mask):

    def per_device(totals, item):
        tile_set, rows_here, cols_here, live_here = item
        sources = blocks[cols_here].astype(jnp.float32)
        products = jnp.einsum('tij,tjd->tid', tile_set.astype(jnp.float32), sources, precision=lax.Precision.HIGHEST)
        products = products * live_here[:, None, None]
        return (totals.at[rows_here].add(products), None)
    totals = jnp.zeros((NODES // BLK, BLK, D), jnp.float32)
    totals, _ = lax.scan(per_device, totals, (tiles, row_block, col_block, live_mask))
    return totals.reshape(NODES, D)

def spread_back(blocks, tiles, row_block, slot_ids, slot_block, live_mask):
    slot_range = jnp.arange(SLOTS, dtype=jnp.int32)

    def per_device(totals, item):
        tile_set, rows_here, slots_here, targets, live_here = item
        sources = blocks[rows_here].astype(jnp.float32)
        products = jnp.einsum('tji,tjd->tid', tile_set.astype(jnp.float32), sources, precision=lax.Precision.HIGHEST)
        placing = (slots_here[:, None] == slot_range[None, :]).astype(jnp.float32) * live_here[:, None]
        per_slot = jnp.einsum('ts,tid->sid', placing, products, precision=lax.Precision.HIGHEST)
        rounded = lax.optimization_barrier(per_slot.astype(jnp.bfloat16))
        return (totals.at[targets].add(rounded.astype(jnp.float32)), None)
    totals = jnp.zeros((NODES // BLK, BLK, D), jnp.float32)
    totals, _ = lax.scan(per_device, totals, (tiles, row_block, slot_ids, slot_block, live_mask))
    return totals.reshape(NODES, D)

def reference(feats, tile_vals, tile_rows, tile_slots, tile_count, send_list, w_in, w_out, cotangent):
    row_block, col_block, slot_ids, slot_block, live_mask = tile_maps(tile_rows, tile_slots, tile_count, send_list)
    tiles = tile_vals.reshape(DEVICES, TMAX, BLK, BLK)
    hidden = feats
    saved = []
    for layer in range(LAYERS):
        message = aggregate(hidden.reshape(NODES // BLK, BLK, D), tiles, row_block, col_block, live_mask)
        summed = message + hidden.astype(jnp.float32)
        norm_scale = lax.rsqrt(lax.optimization_barrier(jnp.mean(summed * summed, axis=-1, keepdims=True)) + eps)
        normed = summed * norm_scale
        normed_b = normed.astype(jnp.bfloat16)
        pre_act = jnp.dot(normed_b, w_in[layer], preferred_element_type=jnp.float32)
        activated = jax.nn.silu(pre_act).astype(jnp.bfloat16)
        update = jnp.dot(activated, w_out[layer], preferred_element_type=jnp.float32)
        saved.append((norm_scale, normed, normed_b, pre_act, activated))
        hidden = (hidden.astype(jnp.float32) + update).astype(jnp.bfloat16)
    grad_now = cotangent
    in_grads = []
    out_grads = []
    for layer in reversed(range(LAYERS)):
        norm_scale, normed, normed_b, pre_act, activated = saved[layer]
        out_grads.append(jnp.dot(activated.T, grad_now, preferred_element_type=jnp.float32))
        d_act = jnp.dot(grad_now, w_out[layer].T, preferred_element_type=jnp.float32)
        sigma = jax.nn.sigmoid(pre_act)
        d_pre = (d_act * sigma * (1.0 + pre_act * (1.0 - sigma))).astype(jnp.bfloat16)
        in_grads.append(jnp.dot(normed_b.T, d_pre, preferred_element_type=jnp.float32))
        d_unit = jnp.dot(d_pre, w_in[layer].T, preferred_element_type=jnp.float32)
        d_summed = norm_scale * (d_unit - normed * lax.optimization_barrier(jnp.mean(d_unit * normed, axis=-1, keepdims=True)))
        d_summed_b = d_summed.astype(jnp.bfloat16)
        returned = spread_back(d_summed_b.reshape(NODES // BLK, BLK, D), tiles, row_block, slot_ids, slot_block, live_mask)
        grad_now = (grad_now.astype(jnp.float32) + d_summed + returned).astype(jnp.bfloat16)
    factor = float(NODES) ** (-0.5)
    w_in_grad = jnp.stack(in_grads[::-1]) * factor
    w_out_grad = jnp.stack(out_grads[::-1]) * factor
    return (grad_now, w_in_grad, w_out_grad)
```

```python
import functools

import jax
import jax.numpy as jnp
from jax import lax
from jax.experimental import pallas as pl
from jax.experimental.pallas import tpu as pltpu
from jax.sharding import Mesh
from jax.sharding import PartitionSpec as P

ROW = ("row_0", "row_1", "row_2")
GRP_ROW = ("grp", "row_0", "row_1", "row_2")
FAR = ("grp", "row_0", "row_1")
NEAR = "row_2"

eps = 1e-06
UNROLL = 4


def exchange(value, axis):
    return lax.all_to_all(value, axis, split_axis=0, concat_axis=0, tiled=True)


def pair_table(keys, key_count, sources, count):
    tile_cap = keys.shape[0]
    steps = -(-((tile_cap + key_count) // 2) // UNROLL) * UNROLL
    ids = jnp.arange(tile_cap, dtype=jnp.int32)
    key_ids = jnp.arange(key_count, dtype=jnp.int32)
    live = ids < count
    held = (keys[:, None] == key_ids[None, :]) & live[:, None]
    per_key = jnp.sum(held.astype(jnp.int32), axis=0)
    per_key_steps = (per_key + 1) // 2
    start = jnp.sum(jnp.where(key_ids[None, :] < key_ids[:, None], per_key_steps[None, :], 0), axis=1)
    before = (keys[:, None] == keys[None, :]) & (ids[None, :] < ids[:, None])
    rank = jnp.sum(before.astype(jnp.int32), axis=1)
    place = 2 * jnp.sum(jnp.where(held, start[None, :], 0), axis=1) + rank
    spots = jnp.arange(2 * steps, dtype=jnp.int32)
    hit = (place[None, :] == spots[:, None]) & live[None, :]
    tile_at = jnp.min(jnp.where(hit, ids[None, :], tile_cap), axis=1)
    source_at = jnp.max(jnp.where(hit, sources[None, :], 0), axis=1)
    step_ids = jnp.arange(steps, dtype=jnp.int32)
    total = jnp.sum(per_key_steps)
    target = jnp.sum((start[None, :] <= step_ids[:, None]).astype(jnp.int32), axis=1) - 1
    target = jnp.where(step_ids < total, target, key_count)
    first = jnp.max((start[None, :] == step_ids[:, None]).astype(jnp.int32), axis=1)
    first = jnp.where(step_ids < total, first, 1)
    turns = (total + UNROLL - 1) // UNROLL
    return jnp.concatenate([tile_at, source_at, target, first, turns[None]]), steps


def tiles_kernel(table, data, tiles, out, tile_buf, acc, sem, *, steps, transposed):
    tile_cap, tile_len, _ = tiles.shape
    out_count = out.shape[0]
    copy = pltpu.make_async_copy(tiles, tile_buf.at[pl.ds(0, tile_cap)], sem)
    copy.start()
    tile_buf[tile_cap] = jnp.zeros((tile_len, tile_len), tile_buf.dtype)
    copy.wait()

    def turn(index, carry):
        products = []
        for u in range(UNROLL):
            step = index * UNROLL + u
            tile_0 = tile_buf[table[2 * step]]
            tile_1 = tile_buf[table[2 * step + 1]]
            data_0 = data[table[2 * steps + 2 * step]]
            data_1 = data[table[2 * steps + 2 * step + 1]]
            values = jnp.concatenate([data_0, data_1], axis=0)
            if transposed:
                pair = jnp.concatenate([tile_0, tile_1], axis=0)
                dims = (((0,), (0,)), ((), ()))
            else:
                pair = jnp.concatenate([tile_0, tile_1], axis=1)
                dims = (((1,), (0,)), ((), ()))
            products.append(
                lax.dot_general(pair, values, dims, preferred_element_type=jnp.float32)
            )
        for u in range(UNROLL):
            step = index * UNROLL + u
            target = table[4 * steps + step]
            first = table[5 * steps + step]
            acc[target] = jnp.where(first == 1, 0.0, acc[target]) + products[u]
        return carry

    lax.fori_loop(0, table[6 * steps], turn, 0)

    def finish(index, carry):
        out[index] = acc[index].astype(out.dtype)
        return carry

    lax.fori_loop(0, out_count, finish, 0)


def run_tiles(table, steps, data, tiles, out_count, transposed):
    tile_cap, tile_len, _ = tiles.shape
    width = data.shape[2]
    return pl.pallas_call(
        functools.partial(tiles_kernel, steps=steps, transposed=transposed),
        out_shape=jax.ShapeDtypeStruct((out_count, tile_len, width), jnp.bfloat16),
        in_specs=[
            pl.BlockSpec(memory_space=pltpu.SMEM),
            pl.BlockSpec(memory_space=pltpu.VMEM),
            pl.BlockSpec(memory_space=pl.ANY),
        ],
        out_specs=pl.BlockSpec(memory_space=pltpu.VMEM),
        scratch_shapes=[
            pltpu.VMEM((tile_cap + 1, tile_len, tile_len), tiles.dtype),
            pltpu.VMEM((out_count + 1, tile_len, width), jnp.float32),
            pltpu.SemaphoreType.DMA,
        ],
        name="tiles_t" if transposed else "tiles",
    )(table, data, tiles)


def pick_kernel(choice, own, out, sems):
    count = out.shape[0]
    copies = [
        pltpu.make_async_copy(own.at[choice[s]], out.at[s], sems.at[s]) for s in range(count)
    ]
    for copy in copies:
        copy.start()
    for copy in copies:
        copy.wait()


def pick_blocks(choice, own):
    count = choice.shape[0]
    return pl.pallas_call(
        pick_kernel,
        out_shape=jax.ShapeDtypeStruct((count, *own.shape[1:]), own.dtype),
        in_specs=[
            pl.BlockSpec(memory_space=pltpu.SMEM),
            pl.BlockSpec(memory_space=pltpu.VMEM),
        ],
        out_specs=pl.BlockSpec(memory_space=pl.ANY),
        scratch_shapes=[pltpu.SemaphoreType.DMA((count,))],
        name="pick",
    )(choice, own)


def place_kernel(choice, returned, base, extra, out, acc):
    acc[...] = base[...].astype(jnp.float32) + extra[...]

    def add(index, carry):
        block = choice[index]
        acc[block] += returned[index].astype(jnp.float32)
        return carry

    lax.fori_loop(0, returned.shape[0], add, 0, unroll=4)
    out[...] = acc[...].astype(out.dtype)


def place_blocks(choice, returned, base, extra):
    return pl.pallas_call(
        place_kernel,
        out_shape=jax.ShapeDtypeStruct(base.shape, base.dtype),
        in_specs=[
            pl.BlockSpec(memory_space=pltpu.SMEM),
            pl.BlockSpec(memory_space=pltpu.VMEM),
            pl.BlockSpec(memory_space=pltpu.VMEM),
            pl.BlockSpec(memory_space=pltpu.VMEM),
        ],
        out_specs=pl.BlockSpec(memory_space=pltpu.VMEM),
        scratch_shapes=[pltpu.VMEM(base.shape, jnp.float32)],
        name="place",
    )(choice, returned, base, extra)


def reduce_weights(value):
    near = lax.axis_size(NEAR)
    far = lax.axis_size(FAR)
    rows, cols = value.shape
    own_rows = rows // (near * far)
    parts = value.reshape(far, near, own_rows, cols).transpose(1, 0, 2, 3)
    parts = exchange(parts.astype(jnp.bfloat16), NEAR)
    nearer = parts.astype(jnp.float32).sum(axis=0)
    arrived = exchange(nearer.astype(jnp.bfloat16), FAR)
    return arrived.astype(jnp.float32).sum(axis=0)


def body(feats, tile_vals, tile_rows, tile_slots, tile_count, send_list, w_in, w_out, cotangent):
    row_count = lax.axis_size(ROW)
    grp_count = lax.axis_size("grp")
    node_count, width = feats.shape
    tile_len = tile_vals.shape[1]
    per_dev = node_count // tile_len
    slot_count = row_count
    panel_len = grp_count * per_dev
    layer_count = w_in.shape[0]
    count = tile_count[0]
    outgoing = send_list[0].reshape(slot_count)
    row_table, row_steps = pair_table(tile_rows, panel_len, tile_slots, count)
    slot_table, slot_steps = pair_table(tile_slots, slot_count, tile_rows, count)
    factor = float(node_count * lax.axis_size(GRP_ROW)) ** (-0.5)
    contract_rows = (((0,), (0,)), ((), ()))
    contract_cols = (((1,), (1,)), ((), ()))
    hidden = feats
    saved = []
    for layer in range(layer_count):
        own_blocks = hidden.reshape(per_dev, tile_len, width)
        slot_data = exchange(pick_blocks(outgoing, own_blocks), ROW)
        partial_value = run_tiles(row_table, row_steps, slot_data, tile_vals, panel_len, False)
        arrived = exchange(partial_value.reshape(grp_count, node_count, width), "grp")
        message = arrived.astype(jnp.float32).sum(axis=0)
        summed = message + hidden.astype(jnp.float32)
        norm_scale = lax.rsqrt(jnp.mean(summed * summed, axis=-1, keepdims=True) + eps)
        normed = summed * norm_scale
        normed_b = normed.astype(jnp.bfloat16)
        pre_act = jnp.dot(normed_b, w_in[layer], preferred_element_type=jnp.float32)
        activated = jax.nn.silu(pre_act).astype(jnp.bfloat16)
        update = jnp.dot(activated, w_out[layer], preferred_element_type=jnp.float32)
        saved.append((norm_scale, normed, normed_b, pre_act, activated))
        hidden = (hidden.astype(jnp.float32) + update).astype(jnp.bfloat16)
    grad_now = cotangent
    in_sums = [None] * layer_count
    out_sums = [None] * layer_count
    for layer in reversed(range(layer_count)):
        norm_scale, normed, normed_b, pre_act, activated = saved[layer]
        out_term = lax.dot_general(
            activated, grad_now, contract_rows, preferred_element_type=jnp.float32
        )
        d_act = lax.dot_general(
            grad_now, w_out[layer], contract_cols, preferred_element_type=jnp.float32
        )
        sigma = jax.nn.sigmoid(pre_act)
        d_pre = (d_act * sigma * (1.0 + pre_act * (1.0 - sigma))).astype(jnp.bfloat16)
        in_term = lax.dot_general(
            normed_b, d_pre, contract_rows, preferred_element_type=jnp.float32
        )
        in_sums[layer] = reduce_weights(in_term)
        out_sums[layer] = reduce_weights(out_term)
        d_unit = lax.dot_general(
            d_pre, w_in[layer], contract_cols, preferred_element_type=jnp.float32
        )
        d_summed = norm_scale * (
            d_unit - normed * jnp.mean(d_unit * normed, axis=-1, keepdims=True)
        )
        d_summed_b = d_summed.astype(jnp.bfloat16)
        panel_grad = exchange(
            jnp.broadcast_to(d_summed_b[None], (grp_count, node_count, width)), "grp"
        ).reshape(panel_len, tile_len, width)
        per_slot = run_tiles(slot_table, slot_steps, panel_grad, tile_vals, slot_count, True)
        returned = exchange(per_slot, ROW)
        block_dims = (per_dev, tile_len, width)
        grad_now = place_blocks(
            outgoing, returned, grad_now.reshape(block_dims), d_summed.reshape(block_dims)
        ).reshape(node_count, width)
    w_in_grad = jnp.stack(in_sums) * factor
    w_out_grad = jnp.stack(out_sums) * factor
    return (grad_now, w_in_grad, w_out_grad)


def solution(mesh):
    torus = Mesh(
        mesh.devices.reshape(mesh.shape["grp"], 4, 4, 2), ("grp", "row_0", "row_1", "row_2")
    )
    in_specs = (
        P(GRP_ROW, None),
        P(GRP_ROW, None, None),
        P(GRP_ROW),
        P(GRP_ROW),
        P(GRP_ROW),
        P(GRP_ROW, None, None),
        P(),
        P(),
        P(GRP_ROW, None),
    )
    out_specs = (P(GRP_ROW, None), P(None, GRP_ROW, None), P(None, GRP_ROW, None))
    return jax.shard_map(body, mesh=torus, in_specs=in_specs, out_specs=out_specs, check_vma=False)
```

```python
import functools

import jax
import jax.numpy as jnp
from jax import lax
from jax.experimental import pallas as pl
from jax.experimental.pallas import tpu as pltpu
from jax.sharding import Mesh
from jax.sharding import PartitionSpec as P

ROW = ("row_0", "row_1", "row_2")
GRP_ROW = ("grp", "row_0", "row_1", "row_2")
FAR = ("grp", "row_0", "row_1")
NEAR = "row_2"

eps = 1e-06
UNROLL = 4
CHUNKS = 2


def exchange(value, axis):
    return lax.all_to_all(value, axis, split_axis=0, concat_axis=0, tiled=True)


def pair_table(keys, key_count, sources, count):
    tile_cap = keys.shape[0]
    steps = -(-((tile_cap + key_count) // 2) // UNROLL) * UNROLL
    ids = jnp.arange(tile_cap, dtype=jnp.int32)
    key_ids = jnp.arange(key_count, dtype=jnp.int32)
    live = ids < count
    held = (keys[:, None] == key_ids[None, :]) & live[:, None]
    per_key = jnp.sum(held.astype(jnp.int32), axis=0)
    per_key_steps = (per_key + 1) // 2
    start = jnp.sum(jnp.where(key_ids[None, :] < key_ids[:, None], per_key_steps[None, :], 0), axis=1)
    before = (keys[:, None] == keys[None, :]) & (ids[None, :] < ids[:, None])
    rank = jnp.sum(before.astype(jnp.int32), axis=1)
    place = 2 * jnp.sum(jnp.where(held, start[None, :], 0), axis=1) + rank
    spots = jnp.arange(2 * steps, dtype=jnp.int32)
    hit = (place[None, :] == spots[:, None]) & live[None, :]
    tile_at = jnp.min(jnp.where(hit, ids[None, :], tile_cap), axis=1)
    source_at = jnp.max(jnp.where(hit, sources[None, :], 0), axis=1)
    step_ids = jnp.arange(steps, dtype=jnp.int32)
    total = jnp.sum(per_key_steps)
    target = jnp.sum((start[None, :] <= step_ids[:, None]).astype(jnp.int32), axis=1) - 1
    target = jnp.where(step_ids < total, target, key_count)
    first = jnp.max((start[None, :] == step_ids[:, None]).astype(jnp.int32), axis=1)
    first = jnp.where(step_ids < total, first, 1)
    turns = (total + UNROLL - 1) // UNROLL
    return jnp.concatenate([tile_at, source_at, target, first, turns[None]]), steps


def tiles_kernel(table, *refs, steps, transposed, piece_count, out_pieces):
    data_pieces = refs[:piece_count]
    tiles = refs[piece_count]
    outs = refs[piece_count + 1 : piece_count + 1 + out_pieces]
    data, tile_buf, acc, data_sems, tile_sem = refs[piece_count + 1 + out_pieces :]
    tile_cap, tile_len, _ = tiles.shape
    piece_len = data_pieces[0].shape[0]
    out_len = outs[0].shape[0]
    copies = [
        pltpu.make_async_copy(
            data_pieces[i], data.at[pl.ds(i * piece_len, piece_len)], data_sems.at[i]
        )
        for i in range(piece_count)
    ]
    copies.append(pltpu.make_async_copy(tiles, tile_buf.at[pl.ds(0, tile_cap)], tile_sem))
    for copy in copies:
        copy.start()
    tile_buf[tile_cap] = jnp.zeros((tile_len, tile_len), tile_buf.dtype)
    for copy in copies:
        copy.wait()

    def turn(index, carry):
        products = []
        for u in range(UNROLL):
            step = index * UNROLL + u
            tile_0 = tile_buf[table[2 * step]]
            tile_1 = tile_buf[table[2 * step + 1]]
            data_0 = data[table[2 * steps + 2 * step]]
            data_1 = data[table[2 * steps + 2 * step + 1]]
            values = jnp.concatenate([data_0, data_1], axis=0)
            if transposed:
                pair = jnp.concatenate([tile_0, tile_1], axis=0)
                dims = (((0,), (0,)), ((), ()))
            else:
                pair = jnp.concatenate([tile_0, tile_1], axis=1)
                dims = (((1,), (0,)), ((), ()))
            products.append(
                lax.dot_general(pair, values, dims, preferred_element_type=jnp.float32)
            )
        for u in range(UNROLL):
            step = index * UNROLL + u
            target = table[4 * steps + step]
            first = table[5 * steps + step]
            acc[target] = jnp.where(first == 1, 0.0, acc[target]) + products[u]
        return carry

    lax.fori_loop(0, table[6 * steps], turn, 0)

    for piece in range(out_pieces):

        def finish(index, carry, piece=piece):
            outs[piece][index] = acc[piece * out_len + index].astype(outs[piece].dtype)
            return carry

        lax.fori_loop(0, out_len, finish, 0, unroll=2)


def run_tiles(table, steps, pieces, tiles, out_count, out_pieces, transposed):
    tile_cap, tile_len, _ = tiles.shape
    piece_len, _, width = pieces[0].shape
    out_len = out_count // out_pieces
    return pl.pallas_call(
        functools.partial(
            tiles_kernel,
            steps=steps,
            transposed=transposed,
            piece_count=len(pieces),
            out_pieces=out_pieces,
        ),
        out_shape=[jax.ShapeDtypeStruct((out_len, tile_len, width), jnp.bfloat16)] * out_pieces,
        in_specs=[pl.BlockSpec(memory_space=pltpu.SMEM)]
        + [pl.BlockSpec(memory_space=pl.ANY)] * (len(pieces) + 1),
        out_specs=[pl.BlockSpec(memory_space=pltpu.VMEM)] * out_pieces,
        scratch_shapes=[
            pltpu.VMEM((piece_len * len(pieces), tile_len, width), jnp.bfloat16),
            pltpu.VMEM((tile_cap + 1, tile_len, tile_len), tiles.dtype),
            pltpu.VMEM((out_count + 1, tile_len, width), jnp.float32),
            pltpu.SemaphoreType.DMA((len(pieces),)),
            pltpu.SemaphoreType.DMA,
        ],
        name="tiles_t" if transposed else "tiles",
    )(table, *pieces, tiles)


def pick_kernel(choice, own, out, sems):
    count = out.shape[0]
    copies = [
        pltpu.make_async_copy(own.at[choice[s]], out.at[s], sems.at[s]) for s in range(count)
    ]
    for copy in copies:
        copy.start()
    for copy in copies:
        copy.wait()


def pick_blocks(choice, own, chunk, width):
    count = choice.shape[0]
    blocks, tile_len, _ = own.shape
    return pl.pallas_call(
        pick_kernel,
        grid=(1,),
        out_shape=jax.ShapeDtypeStruct((count, tile_len, width), own.dtype),
        in_specs=[
            pl.BlockSpec(memory_space=pltpu.SMEM),
            pl.BlockSpec((blocks, tile_len, width), lambda i: (0, 0, chunk)),
        ],
        out_specs=pl.BlockSpec(memory_space=pl.ANY),
        scratch_shapes=[pltpu.SemaphoreType.DMA((count,))],
        name="pick",
    )(choice, own)


def place_kernel(choice, returned, base, extra, out, acc):
    acc[...] = base[...].astype(jnp.float32) + extra[...]

    def add(index, carry):
        block = choice[index]
        acc[block] += returned[index].astype(jnp.float32)
        return carry

    lax.fori_loop(0, returned.shape[0], add, 0, unroll=4)
    out[...] = acc[...].astype(out.dtype)


def place_blocks(choice, returned, base, extra, chunk):
    count, tile_len, width = returned.shape
    block = (base.shape[0], tile_len, width)
    return pl.pallas_call(
        place_kernel,
        grid=(1,),
        out_shape=jax.ShapeDtypeStruct(block, base.dtype),
        in_specs=[
            pl.BlockSpec(memory_space=pltpu.SMEM),
            pl.BlockSpec((count, tile_len, width), lambda i: (0, 0, 0)),
            pl.BlockSpec(block, lambda i: (0, 0, chunk)),
            pl.BlockSpec(block, lambda i: (0, 0, chunk)),
        ],
        out_specs=pl.BlockSpec(block, lambda i: (0, 0, 0)),
        scratch_shapes=[pltpu.VMEM(block, jnp.float32)],
        name="place",
    )(choice, returned, base, extra)


def shifted(value, axis, step):
    length = lax.axis_size(axis)
    return lax.ppermute(value, axis, [(i, (i + step) % length) for i in range(length)])


def reduce_weights(in_term, out_term):
    near = lax.axis_size(NEAR)
    far = lax.axis_size(FAR)
    devices = near * far
    lanes = 128
    flat = [
        term.astype(jnp.bfloat16).reshape(far, near, -1, lanes) for term in (in_term, out_term)
    ]
    parts = jnp.concatenate(flat, axis=2).transpose(1, 0, 2, 3)
    parts = exchange(parts, NEAR)
    nearer = parts.astype(jnp.float32).sum(axis=0)
    arrived = exchange(nearer.astype(jnp.bfloat16), FAR)
    total = arrived.astype(jnp.float32).sum(axis=0)
    split = in_term.size // devices // lanes
    return (
        total[:split].reshape(in_term.shape[0] // devices, in_term.shape[1]),
        total[split:].reshape(out_term.shape[0] // devices, out_term.shape[1]),
    )


def body(feats, tile_vals, tile_rows, tile_slots, tile_count, send_list, w_in, w_out, cotangent):
    row_count = lax.axis_size(ROW)
    grp_count = lax.axis_size("grp")
    node_count, width = feats.shape
    tile_len = tile_vals.shape[1]
    per_dev = node_count // tile_len
    slot_count = row_count
    panel_len = grp_count * per_dev
    layer_count = w_in.shape[0]
    count = tile_count[0]
    outgoing = send_list[0].reshape(slot_count)
    chunk_width = width // CHUNKS
    grp_id = lax.axis_index("grp")
    near_rows = (tile_rows // per_dev - grp_id) % grp_count * per_dev + tile_rows % per_dev
    row_table, row_steps = pair_table(near_rows, panel_len, tile_slots, count)
    slot_table, slot_steps = pair_table(tile_slots, slot_count, near_rows, count)
    factor = float(node_count * lax.axis_size(GRP_ROW)) ** (-0.5)
    contract_rows = (((0,), (0,)), ((), ()))
    contract_cols = (((1,), (1,)), ((), ()))
    hidden = feats
    saved = []
    for layer in range(layer_count):
        own_blocks = hidden.reshape(per_dev, tile_len, width)
        messages = []
        for chunk in range(CHUNKS):
            slot_data = exchange(pick_blocks(outgoing, own_blocks, chunk, chunk_width), ROW)
            pieces = run_tiles(
                row_table, row_steps, [slot_data], tile_vals, panel_len, grp_count, False
            )
            total = pieces[0].astype(jnp.float32)
            for step in (2, 1, 3):
                total = total + shifted(pieces[step], "grp", step).astype(jnp.float32)
            messages.append(total.reshape(node_count, chunk_width))
        message = jnp.concatenate(messages, axis=1)
        summed = message + hidden.astype(jnp.float32)
        norm_scale = lax.rsqrt(jnp.mean(summed * summed, axis=-1, keepdims=True) + eps)
        normed = summed * norm_scale
        normed_b = normed.astype(jnp.bfloat16)
        pre_act = jnp.dot(normed_b, w_in[layer], preferred_element_type=jnp.float32)
        activated = jax.nn.silu(pre_act).astype(jnp.bfloat16)
        update = jnp.dot(activated, w_out[layer], preferred_element_type=jnp.float32)
        saved.append((norm_scale, normed, normed_b, pre_act, activated))
        hidden = (hidden.astype(jnp.float32) + update).astype(jnp.bfloat16)
    grad_now = cotangent
    in_sums = [None] * layer_count
    out_sums = [None] * layer_count
    for layer in reversed(range(layer_count)):
        norm_scale, normed, normed_b, pre_act, activated = saved[layer]
        out_term = lax.dot_general(
            activated, grad_now, contract_rows, preferred_element_type=jnp.float32
        )
        d_act = lax.dot_general(
            grad_now, w_out[layer], contract_cols, preferred_element_type=jnp.float32
        )
        sigma = jax.nn.sigmoid(pre_act)
        d_pre = (d_act * sigma * (1.0 + pre_act * (1.0 - sigma))).astype(jnp.bfloat16)
        in_term = lax.dot_general(
            normed_b, d_pre, contract_rows, preferred_element_type=jnp.float32
        )
        in_sums[layer], out_sums[layer] = reduce_weights(in_term, out_term)
        d_unit = lax.dot_general(
            d_pre, w_in[layer], contract_cols, preferred_element_type=jnp.float32
        )
        d_summed = norm_scale * (
            d_unit - normed * jnp.mean(d_unit * normed, axis=-1, keepdims=True)
        )
        d_summed_b = d_summed.astype(jnp.bfloat16)
        block_dims = (per_dev, tile_len, width)
        grad_blocks = grad_now.reshape(block_dims)
        d_blocks = d_summed.reshape(block_dims)
        d_blocks_b = d_summed_b.reshape(block_dims)
        updated = []
        for chunk in range(CHUNKS):
            own = d_blocks_b[:, :, chunk * chunk_width : (chunk + 1) * chunk_width]
            pieces = [own] + [shifted(own, "grp", grp_count - step) for step in range(1, grp_count)]
            per_slot = run_tiles(slot_table, slot_steps, pieces, tile_vals, slot_count, 1, True)[0]
            returned = exchange(per_slot, ROW)
            updated.append(place_blocks(outgoing, returned, grad_blocks, d_blocks, chunk))
        grad_now = jnp.concatenate(updated, axis=2).reshape(node_count, width)
    w_in_grad = jnp.stack(in_sums) * factor
    w_out_grad = jnp.stack(out_sums) * factor
    return (grad_now, w_in_grad, w_out_grad)


def solution(mesh):
    torus = Mesh(
        mesh.devices.reshape(mesh.shape["grp"], 4, 4, 2), ("grp", "row_0", "row_1", "row_2")
    )
    in_specs = (
        P(GRP_ROW, None),
        P(GRP_ROW, None, None),
        P(GRP_ROW),
        P(GRP_ROW),
        P(GRP_ROW),
        P(GRP_ROW, None, None),
        P(),
        P(),
        P(GRP_ROW, None),
    )
    out_specs = (P(GRP_ROW, None), P(None, GRP_ROW, None), P(None, GRP_ROW, None))
    return jax.shard_map(body, mesh=torus, in_specs=in_specs, out_specs=out_specs, check_vma=False)
```

```python
import functools

import jax
import jax.numpy as jnp
from jax import lax
from jax.experimental import pallas as pl
from jax.experimental.pallas import tpu as pltpu
from jax.sharding import Mesh
from jax.sharding import PartitionSpec as P

ROW = ("row_0", "row_1", "row_2")
GRP_ROW = ("grp", "row_0", "row_1", "row_2")
FAR = ("grp", "row_0", "row_1")
NEAR = "row_2"

eps = 1e-06
UNROLL = 4
CHUNKS = 2


def exchange(value, axis):
    return lax.all_to_all(value, axis, split_axis=0, concat_axis=0, tiled=True)


def pair_table(keys, key_count, sources, count):
    tile_cap = keys.shape[0]
    steps = -(-((tile_cap + key_count) // 2) // UNROLL) * UNROLL
    ids = jnp.arange(tile_cap, dtype=jnp.int32)
    key_ids = jnp.arange(key_count, dtype=jnp.int32)
    live = ids < count
    held = (keys[:, None] == key_ids[None, :]) & live[:, None]
    per_key = jnp.sum(held.astype(jnp.int32), axis=0)
    per_key_steps = (per_key + 1) // 2
    start = jnp.sum(jnp.where(key_ids[None, :] < key_ids[:, None], per_key_steps[None, :], 0), axis=1)
    before = (keys[:, None] == keys[None, :]) & (ids[None, :] < ids[:, None])
    rank = jnp.sum(before.astype(jnp.int32), axis=1)
    place = 2 * jnp.sum(jnp.where(held, start[None, :], 0), axis=1) + rank
    spots = jnp.arange(2 * steps, dtype=jnp.int32)
    hit = (place[None, :] == spots[:, None]) & live[None, :]
    tile_at = jnp.min(jnp.where(hit, ids[None, :], tile_cap), axis=1)
    source_at = jnp.max(jnp.where(hit, sources[None, :], 0), axis=1)
    step_ids = jnp.arange(steps, dtype=jnp.int32)
    total = jnp.sum(per_key_steps)
    target = jnp.sum((start[None, :] <= step_ids[:, None]).astype(jnp.int32), axis=1) - 1
    target = jnp.where(step_ids < total, target, key_count)
    first = jnp.max((start[None, :] == step_ids[:, None]).astype(jnp.int32), axis=1)
    first = jnp.where(step_ids < total, first, 1)
    turns = (total + UNROLL - 1) // UNROLL
    return jnp.concatenate([tile_at, source_at, target, first, turns[None]]), steps


def tiles_kernel(table, *refs, steps, transposed, piece_count, out_pieces):
    data_pieces = refs[:piece_count]
    tiles = refs[piece_count]
    outs = refs[piece_count + 1 : piece_count + 1 + out_pieces]
    data, tile_buf, acc, data_sems, tile_sem = refs[piece_count + 1 + out_pieces :]
    tile_cap, tile_len, _ = tiles.shape
    piece_len = data_pieces[0].shape[0]
    out_len = outs[0].shape[0]
    copies = [
        pltpu.make_async_copy(
            data_pieces[i], data.at[pl.ds(i * piece_len, piece_len)], data_sems.at[i]
        )
        for i in range(piece_count)
    ]
    copies.append(pltpu.make_async_copy(tiles, tile_buf.at[pl.ds(0, tile_cap)], tile_sem))
    for copy in copies:
        copy.start()
    tile_buf[tile_cap] = jnp.zeros((tile_len, tile_len), tile_buf.dtype)
    for copy in copies:
        copy.wait()

    def turn(index, carry):
        products = []
        for u in range(UNROLL):
            step = index * UNROLL + u
            tile_0 = tile_buf[table[2 * step]]
            tile_1 = tile_buf[table[2 * step + 1]]
            data_0 = data[table[2 * steps + 2 * step]]
            data_1 = data[table[2 * steps + 2 * step + 1]]
            values = jnp.concatenate([data_0, data_1], axis=0)
            if transposed:
                pair = jnp.concatenate([tile_0, tile_1], axis=0)
                dims = (((0,), (0,)), ((), ()))
            else:
                pair = jnp.concatenate([tile_0, tile_1], axis=1)
                dims = (((1,), (0,)), ((), ()))
            products.append(
                lax.dot_general(pair, values, dims, preferred_element_type=jnp.float32)
            )
        for u in range(UNROLL):
            step = index * UNROLL + u
            target = table[4 * steps + step]
            first = table[5 * steps + step]
            acc[target] = jnp.where(first == 1, 0.0, acc[target]) + products[u]
        return carry

    lax.fori_loop(0, table[6 * steps], turn, 0)

    for piece in range(out_pieces):

        def finish(index, carry, piece=piece):
            outs[piece][index] = acc[piece * out_len + index].astype(outs[piece].dtype)
            return carry

        lax.fori_loop(0, out_len, finish, 0, unroll=2)


def run_tiles(table, steps, pieces, tiles, out_count, out_pieces, transposed):
    tile_cap, tile_len, _ = tiles.shape
    piece_len, _, width = pieces[0].shape
    out_len = out_count // out_pieces
    return pl.pallas_call(
        functools.partial(
            tiles_kernel,
            steps=steps,
            transposed=transposed,
            piece_count=len(pieces),
            out_pieces=out_pieces,
        ),
        out_shape=[jax.ShapeDtypeStruct((out_len, tile_len, width), jnp.bfloat16)] * out_pieces,
        in_specs=[pl.BlockSpec(memory_space=pltpu.SMEM)]
        + [pl.BlockSpec(memory_space=pl.ANY)] * (len(pieces) + 1),
        out_specs=[pl.BlockSpec(memory_space=pltpu.VMEM)] * out_pieces,
        scratch_shapes=[
            pltpu.VMEM((piece_len * len(pieces), tile_len, width), jnp.bfloat16),
            pltpu.VMEM((tile_cap + 1, tile_len, tile_len), tiles.dtype),
            pltpu.VMEM((out_count + 1, tile_len, width), jnp.float32),
            pltpu.SemaphoreType.DMA((len(pieces),)),
            pltpu.SemaphoreType.DMA,
        ],
        name="tiles_t" if transposed else "tiles",
    )(table, *pieces, tiles)


def pick_kernel(choice, own, out, sems):
    count = out.shape[0]
    copies = [
        pltpu.make_async_copy(own.at[choice[s]], out.at[s], sems.at[s]) for s in range(count)
    ]
    for copy in copies:
        copy.start()
    for copy in copies:
        copy.wait()


def pick_blocks(choice, own, chunk, width):
    count = choice.shape[0]
    blocks, tile_len, _ = own.shape
    return pl.pallas_call(
        pick_kernel,
        grid=(1,),
        out_shape=jax.ShapeDtypeStruct((count, tile_len, width), own.dtype),
        in_specs=[
            pl.BlockSpec(memory_space=pltpu.SMEM),
            pl.BlockSpec((blocks, tile_len, width), lambda i: (0, 0, chunk)),
        ],
        out_specs=pl.BlockSpec(memory_space=pl.ANY),
        scratch_shapes=[pltpu.SemaphoreType.DMA((count,))],
        name="pick",
    )(choice, own)


def place_kernel(choice, returned, base, extra, out, acc):
    acc[...] = base[...].astype(jnp.float32) + extra[...]

    def add(index, carry):
        block = choice[index]
        acc[block] += returned[index].astype(jnp.float32)
        return carry

    lax.fori_loop(0, returned.shape[0], add, 0, unroll=4)
    out[...] = acc[...].astype(out.dtype)


def place_blocks(choice, returned, base, extra, chunk):
    count, tile_len, width = returned.shape
    block = (base.shape[0], tile_len, width)
    return pl.pallas_call(
        place_kernel,
        grid=(1,),
        out_shape=jax.ShapeDtypeStruct(block, base.dtype),
        in_specs=[
            pl.BlockSpec(memory_space=pltpu.SMEM),
            pl.BlockSpec((count, tile_len, width), lambda i: (0, 0, 0)),
            pl.BlockSpec(block, lambda i: (0, 0, chunk)),
            pl.BlockSpec(block, lambda i: (0, 0, chunk)),
        ],
        out_specs=pl.BlockSpec(block, lambda i: (0, 0, 0)),
        scratch_shapes=[pltpu.VMEM(block, jnp.float32)],
        name="place",
    )(choice, returned, base, extra)


def shifted(value, axis, step):
    length = lax.axis_size(axis)
    return lax.ppermute(value, axis, [(i, (i + step) % length) for i in range(length)])


def scatter_sum(value, axis):
    length = lax.axis_size(axis)
    position = lax.axis_index(axis)
    rows = value.shape[0] // length
    total = lax.dynamic_slice_in_dim(value, position * rows, rows, 0)
    for step in range(1, length):
        start = (position + step) % length * rows
        piece = lax.dynamic_slice_in_dim(value, start, rows, 0).astype(jnp.bfloat16)
        total = total + shifted(piece, axis, step).astype(jnp.float32)
    return total


def column_order(columns, parts):
    far = columns // 2 // parts // 4
    place = jnp.arange(columns, dtype=jnp.int32)
    half = place // (columns // 2)
    part = place % (columns // 2) // (far * 4)
    rest = place % (far * 4)
    device = rest // 4 * 2 + (lax.axis_index(NEAR) + half) % 2
    source = (device * parts + part) * 4 + rest % 4
    ids = jnp.arange(columns, dtype=jnp.int32)
    return (ids[:, None] == source[None, :]).astype(jnp.bfloat16)


def reduce_weights(units, d_pre, activated, grad, unit_order, act_order, after):
    contract_rows = (((0,), (0,)), ((), ()))
    ordered_units = jnp.dot(units, unit_order).reshape(units.shape[0], 2, 1, -1)
    ordered_acts = jnp.dot(activated, act_order).reshape(units.shape[0], 2, 2, -1)
    halves = []
    for half in range(2):
        terms = [
            lax.dot_general(left, right, contract_rows, preferred_element_type=jnp.float32)
            for left, right in (
                (ordered_units[:, half, 0], d_pre),
                (ordered_acts[:, half, 0], grad),
                (ordered_acts[:, half, 1], grad),
            )
        ]
        halves.append(jnp.concatenate([term.astype(jnp.bfloat16) for term in terms], axis=1))
    halves[1], _ = lax.optimization_barrier((halves[1], after))
    total = halves[0].astype(jnp.float32) + shifted(halves[1], NEAR, 1).astype(jnp.float32)
    for axis in FAR:
        total = scatter_sum(total, axis)
    width = grad.shape[1]
    hidden_width = d_pre.shape[1]
    out_term = jnp.concatenate(
        [total[:, hidden_width : hidden_width + width], total[:, hidden_width + width :]], axis=0
    )
    return total[:, :hidden_width], out_term


def body(feats, tile_vals, tile_rows, tile_slots, tile_count, send_list, w_in, w_out, cotangent):
    row_count = lax.axis_size(ROW)
    grp_count = lax.axis_size("grp")
    node_count, width = feats.shape
    tile_len = tile_vals.shape[1]
    per_dev = node_count // tile_len
    slot_count = row_count
    panel_len = grp_count * per_dev
    layer_count = w_in.shape[0]
    count = tile_count[0]
    outgoing = send_list[0].reshape(slot_count)
    chunk_width = width // CHUNKS
    grp_id = lax.axis_index("grp")
    near_rows = (tile_rows // per_dev - grp_id) % grp_count * per_dev + tile_rows % per_dev
    row_table, row_steps = pair_table(near_rows, panel_len, tile_slots, count)
    slot_table, slot_steps = pair_table(tile_slots, slot_count, near_rows, count)
    factor = float(node_count * lax.axis_size(GRP_ROW)) ** (-0.5)
    unit_order = column_order(width, 1)
    act_order = column_order(w_in.shape[2], 2)
    contract_cols = (((1,), (1,)), ((), ()))
    hidden = feats
    saved = []
    for layer in range(layer_count):
        own_blocks = hidden.reshape(per_dev, tile_len, width)
        messages = []
        for chunk in range(CHUNKS):
            slot_data = exchange(pick_blocks(outgoing, own_blocks, chunk, chunk_width), ROW)
            pieces = run_tiles(
                row_table, row_steps, [slot_data], tile_vals, panel_len, grp_count, False
            )
            total = pieces[0].astype(jnp.float32)
            for step in (2, 1, 3):
                total = total + shifted(pieces[step], "grp", step).astype(jnp.float32)
            messages.append(total.reshape(node_count, chunk_width))
        message = jnp.concatenate(messages, axis=1)
        summed = message + hidden.astype(jnp.float32)
        norm_scale = lax.rsqrt(jnp.mean(summed * summed, axis=-1, keepdims=True) + eps)
        normed = summed * norm_scale
        normed_b = normed.astype(jnp.bfloat16)
        pre_act = jnp.dot(normed_b, w_in[layer], preferred_element_type=jnp.float32)
        activated = jax.nn.silu(pre_act).astype(jnp.bfloat16)
        update = jnp.dot(activated, w_out[layer], preferred_element_type=jnp.float32)
        saved.append((norm_scale, normed, normed_b, pre_act, activated))
        hidden = (hidden.astype(jnp.float32) + update).astype(jnp.bfloat16)
    grad_now = cotangent
    in_sums = [None] * layer_count
    out_sums = [None] * layer_count
    for layer in reversed(range(layer_count)):
        norm_scale, normed, normed_b, pre_act, activated = saved[layer]
        d_act = lax.dot_general(
            grad_now, w_out[layer], contract_cols, preferred_element_type=jnp.float32
        )
        sigma = jax.nn.sigmoid(pre_act)
        d_pre = (d_act * sigma * (1.0 + pre_act * (1.0 - sigma))).astype(jnp.bfloat16)
        d_unit = lax.dot_general(
            d_pre, w_in[layer], contract_cols, preferred_element_type=jnp.float32
        )
        d_summed = norm_scale * (
            d_unit - normed * jnp.mean(d_unit * normed, axis=-1, keepdims=True)
        )
        d_summed_b, *late = lax.optimization_barrier(
            (d_summed.astype(jnp.bfloat16), normed_b, d_pre, activated, grad_now)
        )
        block_dims = (per_dev, tile_len, width)
        grad_blocks = grad_now.reshape(block_dims)
        d_blocks = d_summed.reshape(block_dims)
        d_blocks_b = d_summed_b.reshape(block_dims)
        updated = []
        for chunk in range(CHUNKS):
            own = d_blocks_b[:, :, chunk * chunk_width : (chunk + 1) * chunk_width]
            if chunk:
                own, _ = lax.optimization_barrier((own, per_slot))
            pieces = [own] + [shifted(own, "grp", grp_count - step) for step in range(1, grp_count)]
            per_slot = run_tiles(slot_table, slot_steps, pieces, tile_vals, slot_count, 1, True)[0]
            if chunk == 0:
                in_sums[layer], out_sums[layer] = reduce_weights(
                    *late, unit_order, act_order, per_slot
                )
            returned = exchange(per_slot, ROW)
            updated.append(place_blocks(outgoing, returned, grad_blocks, d_blocks, chunk))
        grad_now = jnp.concatenate(updated, axis=2).reshape(node_count, width)
    w_in_grad = jnp.stack(in_sums) * factor
    w_out_grad = jnp.stack(out_sums) * factor
    return (grad_now, w_in_grad, w_out_grad)


def solution(mesh):
    torus = Mesh(
        mesh.devices.reshape(mesh.shape["grp"], 4, 4, 2), ("grp", "row_0", "row_1", "row_2")
    )
    in_specs = (
        P(GRP_ROW, None),
        P(GRP_ROW, None, None),
        P(GRP_ROW),
        P(GRP_ROW),
        P(GRP_ROW),
        P(GRP_ROW, None, None),
        P(),
        P(),
        P(GRP_ROW, None),
    )
    out_specs = (P(GRP_ROW, None), P(None, GRP_ROW, None), P(None, GRP_ROW, None))
    return jax.shard_map(body, mesh=torus, in_specs=in_specs, out_specs=out_specs, check_vma=False)
```

```python
import functools

import jax
import jax.numpy as jnp
from jax import lax
from jax.experimental import pallas as pl
from jax.experimental.pallas import tpu as pltpu
from jax.sharding import Mesh
from jax.sharding import PartitionSpec as P

ROW = ("row_0", "row_1", "row_2")
GRP_ROW = ("grp", "row_0", "row_1", "row_2")
FAR = ("grp", "row_0", "row_1")
NEAR = "row_2"

eps = 1e-06
UNROLL = 4
CHUNKS = 2


def exchange(value, axis):
    return lax.all_to_all(value, axis, split_axis=0, concat_axis=0, tiled=True)


def pair_table(keys, key_count, sources, count):
    tile_cap = keys.shape[0]
    steps = -(-((tile_cap + key_count) // 2) // UNROLL) * UNROLL
    ids = jnp.arange(tile_cap, dtype=jnp.int32)
    key_ids = jnp.arange(key_count, dtype=jnp.int32)
    live = ids < count
    held = (keys[:, None] == key_ids[None, :]) & live[:, None]
    per_key = jnp.sum(held.astype(jnp.int32), axis=0)
    per_key_steps = (per_key + 1) // 2
    start = jnp.sum(jnp.where(key_ids[None, :] < key_ids[:, None], per_key_steps[None, :], 0), axis=1)
    before = (keys[:, None] == keys[None, :]) & (ids[None, :] < ids[:, None])
    rank = jnp.sum(before.astype(jnp.int32), axis=1)
    place = 2 * jnp.sum(jnp.where(held, start[None, :], 0), axis=1) + rank
    spots = jnp.arange(2 * steps, dtype=jnp.int32)
    hit = (place[None, :] == spots[:, None]) & live[None, :]
    tile_at = jnp.min(jnp.where(hit, ids[None, :], tile_cap), axis=1)
    source_at = jnp.max(jnp.where(hit, sources[None, :], 0), axis=1)
    step_ids = jnp.arange(steps, dtype=jnp.int32)
    total = jnp.sum(per_key_steps)
    target = jnp.sum((start[None, :] <= step_ids[:, None]).astype(jnp.int32), axis=1) - 1
    target = jnp.where(step_ids < total, target, key_count)
    first = jnp.max((start[None, :] == step_ids[:, None]).astype(jnp.int32), axis=1)
    first = jnp.where(step_ids < total, first, 1)
    turns = (total + UNROLL - 1) // UNROLL
    return jnp.concatenate([tile_at, source_at, target, first, turns[None]]), steps


def tiles_kernel(table, *refs, steps, transposed, piece_count, out_pieces):
    data_pieces = refs[:piece_count]
    tiles = refs[piece_count]
    outs = refs[piece_count + 1 : piece_count + 1 + out_pieces]
    data, tile_buf, acc, data_sems, tile_sem = refs[piece_count + 1 + out_pieces :]
    tile_cap, tile_len, _ = tiles.shape
    piece_len = data_pieces[0].shape[0]
    out_len = outs[0].shape[0]
    copies = [
        pltpu.make_async_copy(
            data_pieces[i], data.at[pl.ds(i * piece_len, piece_len)], data_sems.at[i]
        )
        for i in range(piece_count)
    ]
    copies.append(pltpu.make_async_copy(tiles, tile_buf.at[pl.ds(0, tile_cap)], tile_sem))
    for copy in copies:
        copy.start()
    tile_buf[tile_cap] = jnp.zeros((tile_len, tile_len), tile_buf.dtype)
    for copy in copies:
        copy.wait()

    def turn(index, carry):
        products = []
        for u in range(UNROLL):
            step = index * UNROLL + u
            tile_0 = tile_buf[table[2 * step]]
            tile_1 = tile_buf[table[2 * step + 1]]
            data_0 = data[table[2 * steps + 2 * step]]
            data_1 = data[table[2 * steps + 2 * step + 1]]
            values = jnp.concatenate([data_0, data_1], axis=0)
            if transposed:
                pair = jnp.concatenate([tile_0, tile_1], axis=0)
                dims = (((0,), (0,)), ((), ()))
            else:
                pair = jnp.concatenate([tile_0, tile_1], axis=1)
                dims = (((1,), (0,)), ((), ()))
            products.append(
                lax.dot_general(pair, values, dims, preferred_element_type=jnp.float32)
            )
        for u in range(UNROLL):
            step = index * UNROLL + u
            target = table[4 * steps + step]
            first = table[5 * steps + step]
            acc[target] = jnp.where(first == 1, 0.0, acc[target]) + products[u]
        return carry

    lax.fori_loop(0, table[6 * steps], turn, 0)

    for piece in range(out_pieces):

        def finish(index, carry, piece=piece):
            outs[piece][index] = acc[piece * out_len + index].astype(outs[piece].dtype)
            return carry

        lax.fori_loop(0, out_len, finish, 0, unroll=2)


def run_tiles(table, steps, pieces, tiles, out_count, out_pieces, transposed):
    tile_cap, tile_len, _ = tiles.shape
    piece_len, _, width = pieces[0].shape
    out_len = out_count // out_pieces
    return pl.pallas_call(
        functools.partial(
            tiles_kernel,
            steps=steps,
            transposed=transposed,
            piece_count=len(pieces),
            out_pieces=out_pieces,
        ),
        out_shape=[jax.ShapeDtypeStruct((out_len, tile_len, width), jnp.bfloat16)] * out_pieces,
        in_specs=[pl.BlockSpec(memory_space=pltpu.SMEM)]
        + [pl.BlockSpec(memory_space=pl.ANY)] * (len(pieces) + 1),
        out_specs=[pl.BlockSpec(memory_space=pltpu.VMEM)] * out_pieces,
        scratch_shapes=[
            pltpu.VMEM((piece_len * len(pieces), tile_len, width), jnp.bfloat16),
            pltpu.VMEM((tile_cap + 1, tile_len, tile_len), tiles.dtype),
            pltpu.VMEM((out_count + 1, tile_len, width), jnp.float32),
            pltpu.SemaphoreType.DMA((len(pieces),)),
            pltpu.SemaphoreType.DMA,
        ],
        name="tiles_t" if transposed else "tiles",
    )(table, *pieces, tiles)


def pick_kernel(choice, own, out, sems):
    def copy(slot):
        return pltpu.make_async_copy(own.at[choice[slot]], out.at[slot], sems.at[slot])

    def start(slot, carry):
        copy(slot).start()
        return carry

    def wait(slot, carry):
        copy(slot).wait()
        return carry

    lax.fori_loop(0, out.shape[0], start, 0)
    lax.fori_loop(0, out.shape[0], wait, 0)


def pick_blocks(choice, own, chunk, width):
    count = choice.shape[0]
    blocks, tile_len, _ = own.shape
    return pl.pallas_call(
        pick_kernel,
        grid=(1,),
        out_shape=jax.ShapeDtypeStruct((count, tile_len, width), own.dtype),
        in_specs=[
            pl.BlockSpec(memory_space=pltpu.SMEM),
            pl.BlockSpec((blocks, tile_len, width), lambda i: (0, 0, chunk)),
        ],
        out_specs=pl.BlockSpec(memory_space=pl.ANY),
        scratch_shapes=[pltpu.SemaphoreType.DMA((count,))],
        name="pick",
    )(choice, own)


def place_kernel(choice, returned, base, extra, out, acc):
    acc[...] = base[...].astype(jnp.float32) + extra[...]

    def add(index, carry):
        block = choice[index]
        acc[block] += returned[index].astype(jnp.float32)
        return carry

    lax.fori_loop(0, returned.shape[0], add, 0, unroll=4)
    out[...] = acc[...].astype(out.dtype)


def place_blocks(choice, returned, base, extra, chunk):
    count, tile_len, width = returned.shape
    block = (base.shape[0], tile_len, width)
    return pl.pallas_call(
        place_kernel,
        grid=(1,),
        out_shape=jax.ShapeDtypeStruct(block, base.dtype),
        in_specs=[
            pl.BlockSpec(memory_space=pltpu.SMEM),
            pl.BlockSpec((count, tile_len, width), lambda i: (0, 0, 0)),
            pl.BlockSpec(block, lambda i: (0, 0, chunk)),
            pl.BlockSpec(block, lambda i: (0, 0, chunk)),
        ],
        out_specs=pl.BlockSpec(block, lambda i: (0, 0, 0)),
        scratch_shapes=[pltpu.VMEM(block, jnp.float32)],
        name="place",
    )(choice, returned, base, extra)


def shifted(value, axis, step):
    length = lax.axis_size(axis)
    return lax.ppermute(value, axis, [(i, (i + step) % length) for i in range(length)])


def scatter_sum(value, axis):
    length = lax.axis_size(axis)
    position = lax.axis_index(axis)
    rows = value.shape[0] // length
    total = lax.dynamic_slice_in_dim(value, position * rows, rows, 0)
    for step in range(1, length):
        start = (position + step) % length * rows
        piece = lax.dynamic_slice_in_dim(value, start, rows, 0).astype(jnp.bfloat16)
        total = total + shifted(piece, axis, step).astype(jnp.float32)
    return total


def column_order(columns, parts):
    far = columns // 2 // parts // 4
    place = jnp.arange(columns, dtype=jnp.int32)
    half = place // (columns // 2)
    part = place % (columns // 2) // (far * 4)
    rest = place % (far * 4)
    device = rest // 4 * 2 + (lax.axis_index(NEAR) + half) % 2
    source = (device * parts + part) * 4 + rest % 4
    ids = jnp.arange(columns, dtype=jnp.int32)
    return (ids[:, None] == source[None, :]).astype(jnp.bfloat16)


def reduce_weights(units, d_pre, activated, grad, unit_order, act_order, after):
    contract_rows = (((0,), (0,)), ((), ()))
    ordered_units = jnp.dot(units, unit_order).reshape(units.shape[0], 2, 1, -1)
    ordered_acts = jnp.dot(activated, act_order).reshape(units.shape[0], 2, 2, -1)
    halves = []
    for half in range(2):
        terms = [
            lax.dot_general(left, right, contract_rows, preferred_element_type=jnp.float32)
            for left, right in (
                (ordered_units[:, half, 0], d_pre),
                (ordered_acts[:, half, 0], grad),
                (ordered_acts[:, half, 1], grad),
            )
        ]
        halves.append(jnp.concatenate([term.astype(jnp.bfloat16) for term in terms], axis=1))
    halves[1], _ = lax.optimization_barrier((halves[1], after))
    total = halves[0].astype(jnp.float32) + shifted(halves[1], NEAR, 1).astype(jnp.float32)
    return scatter_sum(total, FAR[0])


def body(feats, tile_vals, tile_rows, tile_slots, tile_count, send_list, w_in, w_out, cotangent):
    row_count = lax.axis_size(ROW)
    grp_count = lax.axis_size("grp")
    node_count, width = feats.shape
    tile_len = tile_vals.shape[1]
    per_dev = node_count // tile_len
    slot_count = row_count
    panel_len = grp_count * per_dev
    layer_count = w_in.shape[0]
    count = tile_count[0]
    outgoing = send_list[0].reshape(slot_count)
    chunk_width = width // CHUNKS
    grp_id = lax.axis_index("grp")
    near_rows = (tile_rows // per_dev - grp_id) % grp_count * per_dev + tile_rows % per_dev
    row_table, row_steps = pair_table(near_rows, panel_len, tile_slots, count)
    slot_table, slot_steps = pair_table(tile_slots, slot_count, near_rows, count)
    factor = float(node_count * lax.axis_size(GRP_ROW)) ** (-0.5)
    unit_order = column_order(width, 1)
    act_order = column_order(w_in.shape[2], 2)
    contract_cols = (((1,), (1,)), ((), ()))
    hidden = feats
    saved = []
    for layer in range(layer_count):
        own_blocks = hidden.reshape(per_dev, tile_len, width)
        messages = []
        for chunk in range(CHUNKS):
            slot_data = exchange(pick_blocks(outgoing, own_blocks, chunk, chunk_width), ROW)
            pieces = run_tiles(
                row_table, row_steps, [slot_data], tile_vals, panel_len, grp_count, False
            )
            total = pieces[0].astype(jnp.float32)
            for step in (2, 1, 3):
                total = total + shifted(pieces[step], "grp", step).astype(jnp.float32)
            messages.append(total.reshape(node_count, chunk_width))
        message = jnp.concatenate(messages, axis=1)
        summed = message + hidden.astype(jnp.float32)
        norm_scale = lax.rsqrt(jnp.mean(summed * summed, axis=-1, keepdims=True) + eps)
        normed = summed * norm_scale
        normed_b = normed.astype(jnp.bfloat16)
        pre_act = jnp.dot(normed_b, w_in[layer], preferred_element_type=jnp.float32)
        activated = jax.nn.silu(pre_act).astype(jnp.bfloat16)
        update = jnp.dot(activated, w_out[layer], preferred_element_type=jnp.float32)
        saved.append((norm_scale, normed, normed_b, pre_act, activated))
        hidden = (hidden.astype(jnp.float32) + update).astype(jnp.bfloat16)
    grad_now = cotangent
    sums = [None] * layer_count
    for layer in reversed(range(layer_count)):
        norm_scale, normed, normed_b, pre_act, activated = saved[layer]
        d_act = lax.dot_general(
            grad_now, w_out[layer], contract_cols, preferred_element_type=jnp.float32
        )
        sigma = jax.nn.sigmoid(pre_act)
        d_pre = (d_act * sigma * (1.0 + pre_act * (1.0 - sigma))).astype(jnp.bfloat16)
        d_unit = lax.dot_general(
            d_pre, w_in[layer], contract_cols, preferred_element_type=jnp.float32
        )
        d_summed = norm_scale * (
            d_unit - normed * jnp.mean(d_unit * normed, axis=-1, keepdims=True)
        )
        d_summed_b, *late = lax.optimization_barrier(
            (d_summed.astype(jnp.bfloat16), normed_b, d_pre, activated, grad_now)
        )
        block_dims = (per_dev, tile_len, width)
        grad_blocks = grad_now.reshape(block_dims)
        d_blocks = d_summed.reshape(block_dims)
        d_blocks_b = d_summed_b.reshape(block_dims)
        updated = []
        for chunk in range(CHUNKS):
            own = d_blocks_b[:, :, chunk * chunk_width : (chunk + 1) * chunk_width]
            if chunk:
                own, _ = lax.optimization_barrier((own, per_slot))
            pieces = [own] + [shifted(own, "grp", grp_count - step) for step in range(1, grp_count)]
            per_slot = run_tiles(slot_table, slot_steps, pieces, tile_vals, slot_count, 1, True)[0]
            if chunk == (CHUNKS - 1 if layer else 0):
                sums[layer] = reduce_weights(
                    *late, unit_order, act_order, per_slot
                )
            returned = exchange(per_slot, ROW)
            updated.append(place_blocks(outgoing, returned, grad_blocks, d_blocks, chunk))
        grad_now = jnp.concatenate(updated, axis=2).reshape(node_count, width)
        if layer:
            grad_now, sums[layer] = lax.optimization_barrier((grad_now, sums[layer]))
    total = jnp.concatenate(sums, axis=1)
    for axis in FAR[1:]:
        total = scatter_sum(total, axis)
    total = total.reshape(total.shape[0], layer_count, -1) * factor
    split = w_in.shape[2]
    w_in_grad = jnp.swapaxes(total[:, :, :split], 0, 1)
    out_parts = total[:, :, split:].reshape(-1, layer_count, 2, width)
    w_out_grad = out_parts.transpose(1, 2, 0, 3).reshape(layer_count, -1, width)
    return (grad_now, w_in_grad, w_out_grad)


def solution(mesh):
    torus = Mesh(
        mesh.devices.reshape(mesh.shape["grp"], 4, 4, 2), ("grp", "row_0", "row_1", "row_2")
    )
    in_specs = (
        P(GRP_ROW, None),
        P(GRP_ROW, None, None),
        P(GRP_ROW),
        P(GRP_ROW),
        P(GRP_ROW),
        P(GRP_ROW, None, None),
        P(),
        P(),
        P(GRP_ROW, None),
    )
    out_specs = (P(GRP_ROW, None), P(None, GRP_ROW, None), P(None, GRP_ROW, None))
    return jax.shard_map(body, mesh=torus, in_specs=in_specs, out_specs=out_specs, check_vma=False)
```

```python
import functools

import jax
import jax.numpy as jnp
from jax import lax
from jax.experimental import pallas as pl
from jax.experimental.pallas import tpu as pltpu
from jax.sharding import Mesh
from jax.sharding import PartitionSpec as P

ROW = ("row_0", "row_1", "row_2")
GRP_ROW = ("grp", "row_0", "row_1", "row_2")
FAR = ("grp", "row_0", "row_1")
NEAR = "row_2"

eps = 1e-06
UNROLL = 4
CHUNKS = 2


def exchange(value, axis):
    return lax.all_to_all(value, axis, split_axis=0, concat_axis=0, tiled=True)


def pair_table(keys, key_count, sources, count):
    tile_cap = keys.shape[0]
    steps = -(-((tile_cap + key_count) // 2) // UNROLL) * UNROLL
    ids = jnp.arange(tile_cap, dtype=jnp.int32)
    key_ids = jnp.arange(key_count, dtype=jnp.int32)
    live = ids < count
    held = (keys[:, None] == key_ids[None, :]) & live[:, None]
    per_key = jnp.sum(held.astype(jnp.int32), axis=0)
    per_key_steps = (per_key + 1) // 2
    start = jnp.sum(jnp.where(key_ids[None, :] < key_ids[:, None], per_key_steps[None, :], 0), axis=1)
    before = (keys[:, None] == keys[None, :]) & (ids[None, :] < ids[:, None])
    rank = jnp.sum(before.astype(jnp.int32), axis=1)
    place = 2 * jnp.sum(jnp.where(held, start[None, :], 0), axis=1) + rank
    spots = jnp.arange(2 * steps, dtype=jnp.int32)
    hit = (place[None, :] == spots[:, None]) & live[None, :]
    tile_at = jnp.min(jnp.where(hit, ids[None, :], tile_cap), axis=1)
    source_at = jnp.max(jnp.where(hit, sources[None, :], 0), axis=1)
    step_ids = jnp.arange(steps, dtype=jnp.int32)
    total = jnp.sum(per_key_steps)
    target = jnp.sum((start[None, :] <= step_ids[:, None]).astype(jnp.int32), axis=1) - 1
    target = jnp.where(step_ids < total, target, key_count)
    first = jnp.max((start[None, :] == step_ids[:, None]).astype(jnp.int32), axis=1)
    first = jnp.where(step_ids < total, first, 1)
    turns = (total + UNROLL - 1) // UNROLL
    return jnp.concatenate([tile_at, source_at, target, first, turns[None]]), steps


def tiles_kernel(table, *refs, steps, transposed, piece_count, out_pieces):
    data_pieces = refs[:piece_count]
    tiles = refs[piece_count]
    outs = refs[piece_count + 1 : piece_count + 1 + out_pieces]
    data, tile_buf, acc, data_sems, tile_sem = refs[piece_count + 1 + out_pieces :]
    tile_cap, tile_len, _ = tiles.shape
    piece_len = data_pieces[0].shape[0]
    out_len = outs[0].shape[0]
    copies = [
        pltpu.make_async_copy(
            data_pieces[i], data.at[pl.ds(i * piece_len, piece_len)], data_sems.at[i]
        )
        for i in range(piece_count)
    ]
    copies.append(pltpu.make_async_copy(tiles, tile_buf.at[pl.ds(0, tile_cap)], tile_sem))
    for copy in copies:
        copy.start()
    tile_buf[tile_cap] = jnp.zeros((tile_len, tile_len), tile_buf.dtype)
    for copy in copies:
        copy.wait()

    def turn(index, carry):
        products = []
        for u in range(UNROLL):
            step = index * UNROLL + u
            tile_0 = tile_buf[table[2 * step]]
            tile_1 = tile_buf[table[2 * step + 1]]
            data_0 = data[table[2 * steps + 2 * step]]
            data_1 = data[table[2 * steps + 2 * step + 1]]
            values = jnp.concatenate([data_0, data_1], axis=0)
            if transposed:
                pair = jnp.concatenate([tile_0, tile_1], axis=0)
                dims = (((0,), (0,)), ((), ()))
            else:
                pair = jnp.concatenate([tile_0, tile_1], axis=1)
                dims = (((1,), (0,)), ((), ()))
            products.append(
                lax.dot_general(pair, values, dims, preferred_element_type=jnp.float32)
            )
        for u in range(UNROLL):
            step = index * UNROLL + u
            target = table[4 * steps + step]
            first = table[5 * steps + step]
            acc[target] = jnp.where(first == 1, 0.0, acc[target]) + products[u]
        return carry

    lax.fori_loop(0, table[6 * steps], turn, 0)

    for piece in range(out_pieces):

        def finish(index, carry, piece=piece):
            outs[piece][index] = acc[piece * out_len + index].astype(outs[piece].dtype)
            return carry

        lax.fori_loop(0, out_len, finish, 0, unroll=2)


def run_tiles(table, steps, pieces, tiles, out_count, out_pieces, transposed):
    tile_cap, tile_len, _ = tiles.shape
    piece_len, _, width = pieces[0].shape
    out_len = out_count // out_pieces
    return pl.pallas_call(
        functools.partial(
            tiles_kernel,
            steps=steps,
            transposed=transposed,
            piece_count=len(pieces),
            out_pieces=out_pieces,
        ),
        out_shape=[jax.ShapeDtypeStruct((out_len, tile_len, width), jnp.bfloat16)] * out_pieces,
        in_specs=[pl.BlockSpec(memory_space=pltpu.SMEM)]
        + [pl.BlockSpec(memory_space=pl.ANY)] * (len(pieces) + 1),
        out_specs=[pl.BlockSpec(memory_space=pltpu.VMEM)] * out_pieces,
        scratch_shapes=[
            pltpu.VMEM((piece_len * len(pieces), tile_len, width), jnp.bfloat16),
            pltpu.VMEM((tile_cap + 1, tile_len, tile_len), tiles.dtype),
            pltpu.VMEM((out_count + 1, tile_len, width), jnp.float32),
            pltpu.SemaphoreType.DMA((len(pieces),)),
            pltpu.SemaphoreType.DMA,
        ],
        name="tiles_t" if transposed else "tiles",
    )(table, *pieces, tiles)


def pick_kernel(choice, own, out, sems):
    def copy(slot):
        return pltpu.make_async_copy(own.at[choice[slot]], out.at[slot], sems.at[slot])

    def start(slot, carry):
        copy(slot).start()
        return carry

    def wait(slot, carry):
        copy(slot).wait()
        return carry

    lax.fori_loop(0, out.shape[0], start, 0)
    lax.fori_loop(0, out.shape[0], wait, 0)


def pick_blocks(choice, own, chunk, width):
    count = choice.shape[0]
    blocks, tile_len, _ = own.shape
    return pl.pallas_call(
        pick_kernel,
        grid=(1,),
        out_shape=jax.ShapeDtypeStruct((count, tile_len, width), own.dtype),
        in_specs=[
            pl.BlockSpec(memory_space=pltpu.SMEM),
            pl.BlockSpec((blocks, tile_len, width), lambda i: (0, 0, chunk)),
        ],
        out_specs=pl.BlockSpec(memory_space=pl.ANY),
        scratch_shapes=[pltpu.SemaphoreType.DMA((count,))],
        name="pick",
    )(choice, own)


def place_kernel(choice, returned, base, extra, out, acc):
    acc[...] = base[...].astype(jnp.float32) + extra[...]

    def add(index, carry):
        block = choice[index]
        acc[block] += returned[index].astype(jnp.float32)
        return carry

    lax.fori_loop(0, returned.shape[0], add, 0, unroll=4)
    out[...] = acc[...].astype(out.dtype)


def place_blocks(choice, returned, base, extra, chunk):
    count, tile_len, width = returned.shape
    block = (base.shape[0], tile_len, width)
    return pl.pallas_call(
        place_kernel,
        grid=(1,),
        out_shape=jax.ShapeDtypeStruct(block, base.dtype),
        in_specs=[
            pl.BlockSpec(memory_space=pltpu.SMEM),
            pl.BlockSpec((count, tile_len, width), lambda i: (0, 0, 0)),
            pl.BlockSpec(block, lambda i: (0, 0, chunk)),
            pl.BlockSpec(block, lambda i: (0, 0, chunk)),
        ],
        out_specs=pl.BlockSpec(block, lambda i: (0, 0, 0)),
        scratch_shapes=[pltpu.VMEM(block, jnp.float32)],
        name="place",
    )(choice, returned, base, extra)


def shifted(value, axis, step):
    length = lax.axis_size(axis)
    return lax.ppermute(value, axis, [(i, (i + step) % length) for i in range(length)])


def scatter_sum(value, axis):
    length = lax.axis_size(axis)
    position = lax.axis_index(axis)
    rows = value.shape[0] // length
    total = lax.dynamic_slice_in_dim(value, position * rows, rows, 0)
    for step in range(1, length):
        start = (position + step) % length * rows
        piece = lax.dynamic_slice_in_dim(value, start, rows, 0).astype(jnp.bfloat16)
        total = total + shifted(piece, axis, step).astype(jnp.float32)
    return total


def column_order(columns, parts):
    far = columns // 2 // parts // 4
    place = jnp.arange(columns, dtype=jnp.int32)
    half = place // (columns // 2)
    part = place % (columns // 2) // (far * 4)
    rest = place % (far * 4)
    device = rest // 4 * 2 + (lax.axis_index(NEAR) + half) % 2
    source = (device * parts + part) * 4 + rest % 4
    ids = jnp.arange(columns, dtype=jnp.int32)
    return (ids[:, None] == source[None, :]).astype(jnp.bfloat16)


def reduce_weights(units, d_pre, activated, grad, unit_order, act_order, after):
    contract_rows = (((0,), (0,)), ((), ()))
    in_term, out_term = [
        lax.dot_general(
            jnp.dot(left, order), right, contract_rows, preferred_element_type=jnp.float32
        ).astype(jnp.bfloat16)
        for left, order, right in ((units, unit_order, d_pre), (activated, act_order, grad))
    ]
    quarter = out_term.shape[0] // 4
    halves = [
        jnp.concatenate(
            [
                in_term[half * quarter : (half + 1) * quarter],
                out_term[2 * half * quarter : (2 * half + 1) * quarter],
                out_term[(2 * half + 1) * quarter : (2 * half + 2) * quarter],
            ],
            axis=1,
        )
        for half in range(2)
    ]
    halves[1], _ = lax.optimization_barrier((halves[1], after))
    total = halves[0].astype(jnp.float32) + shifted(halves[1], NEAR, 1).astype(jnp.float32)
    return scatter_sum(total, FAR[0])


def body(feats, tile_vals, tile_rows, tile_slots, tile_count, send_list, w_in, w_out, cotangent):
    row_count = lax.axis_size(ROW)
    grp_count = lax.axis_size("grp")
    node_count, width = feats.shape
    tile_len = tile_vals.shape[1]
    per_dev = node_count // tile_len
    slot_count = row_count
    panel_len = grp_count * per_dev
    layer_count = w_in.shape[0]
    count = tile_count[0]
    outgoing = send_list[0].reshape(slot_count)
    chunk_width = width // CHUNKS
    grp_id = lax.axis_index("grp")
    near_rows = (tile_rows // per_dev - grp_id) % grp_count * per_dev + tile_rows % per_dev
    row_table, row_steps = pair_table(near_rows, panel_len, tile_slots, count)
    slot_table, slot_steps = pair_table(tile_slots, slot_count, near_rows, count)
    factor = float(node_count * lax.axis_size(GRP_ROW)) ** (-0.5)
    unit_order = column_order(width, 1)
    act_order = column_order(w_in.shape[2], 2)
    contract_cols = (((1,), (1,)), ((), ()))
    hidden = feats
    saved = []
    for layer in range(layer_count):
        own_blocks = hidden.reshape(per_dev, tile_len, width)
        messages = []
        for chunk in range(CHUNKS):
            slot_data = exchange(pick_blocks(outgoing, own_blocks, chunk, chunk_width), ROW)
            pieces = run_tiles(
                row_table, row_steps, [slot_data], tile_vals, panel_len, grp_count, False
            )
            total = pieces[0].astype(jnp.float32)
            for step in (2, 1, 3):
                total = total + shifted(pieces[step], "grp", step).astype(jnp.float32)
            messages.append(total.reshape(node_count, chunk_width))
        message = jnp.concatenate(messages, axis=1)
        summed = message + hidden.astype(jnp.float32)
        norm_scale = lax.rsqrt(jnp.mean(summed * summed, axis=-1, keepdims=True) + eps)
        normed = summed * norm_scale
        normed_b = normed.astype(jnp.bfloat16)
        pre_act = jnp.dot(normed_b, w_in[layer], preferred_element_type=jnp.float32)
        activated = jax.nn.silu(pre_act).astype(jnp.bfloat16)
        update = jnp.dot(activated, w_out[layer], preferred_element_type=jnp.float32)
        saved.append((norm_scale, normed, normed_b, pre_act, activated))
        hidden = (hidden.astype(jnp.float32) + update).astype(jnp.bfloat16)
    grad_now = cotangent
    sums = [None] * layer_count
    for layer in reversed(range(layer_count)):
        norm_scale, normed, normed_b, pre_act, activated = saved[layer]
        d_act = lax.dot_general(
            grad_now, w_out[layer], contract_cols, preferred_element_type=jnp.float32
        )
        sigma = jax.nn.sigmoid(pre_act)
        d_pre = (d_act * sigma * (1.0 + pre_act * (1.0 - sigma))).astype(jnp.bfloat16)
        d_unit = lax.dot_general(
            d_pre, w_in[layer], contract_cols, preferred_element_type=jnp.float32
        )
        d_summed = norm_scale * (
            d_unit - normed * jnp.mean(d_unit * normed, axis=-1, keepdims=True)
        )
        d_summed_b, *late = lax.optimization_barrier(
            (d_summed.astype(jnp.bfloat16), normed_b, d_pre, activated, grad_now)
        )
        block_dims = (per_dev, tile_len, width)
        grad_blocks = grad_now.reshape(block_dims)
        d_blocks = d_summed.reshape(block_dims)
        d_blocks_b = d_summed_b.reshape(block_dims)
        updated = []
        for chunk in range(CHUNKS):
            own = d_blocks_b[:, :, chunk * chunk_width : (chunk + 1) * chunk_width]
            if chunk:
                own, _ = lax.optimization_barrier((own, per_slot))
            pieces = [own] + [shifted(own, "grp", grp_count - step) for step in range(1, grp_count)]
            per_slot = run_tiles(slot_table, slot_steps, pieces, tile_vals, slot_count, 1, True)[0]
            if chunk == (CHUNKS - 1 if layer else 0):
                sums[layer] = reduce_weights(
                    *late, unit_order, act_order, per_slot
                )
            returned = exchange(per_slot, ROW)
            updated.append(place_blocks(outgoing, returned, grad_blocks, d_blocks, chunk))
        grad_now = jnp.concatenate(updated, axis=2).reshape(node_count, width)
        if layer:
            grad_now, sums[layer] = lax.optimization_barrier((grad_now, sums[layer]))
    total = jnp.concatenate(sums, axis=1)
    for axis in FAR[1:]:
        total = scatter_sum(total, axis)
    total = total.reshape(total.shape[0], layer_count, -1) * factor
    split = w_in.shape[2]
    w_in_grad = jnp.swapaxes(total[:, :, :split], 0, 1)
    out_parts = total[:, :, split:].reshape(-1, layer_count, 2, width)
    w_out_grad = out_parts.transpose(1, 2, 0, 3).reshape(layer_count, -1, width)
    return (grad_now, w_in_grad, w_out_grad)


def solution(mesh):
    torus = Mesh(
        mesh.devices.reshape(mesh.shape["grp"], 4, 4, 2), ("grp", "row_0", "row_1", "row_2")
    )
    in_specs = (
        P(GRP_ROW, None),
        P(GRP_ROW, None, None),
        P(GRP_ROW),
        P(GRP_ROW),
        P(GRP_ROW),
        P(GRP_ROW, None, None),
        P(),
        P(),
        P(GRP_ROW, None),
    )
    out_specs = (P(GRP_ROW, None), P(None, GRP_ROW, None), P(None, GRP_ROW, None))
    return jax.shard_map(body, mesh=torus, in_specs=in_specs, out_specs=out_specs, check_vma=False)
```
